256 devices in a mesh: az: 64 (over z, x, y_lo), rad: 2 (over core), ht: 2 (over y_hi).
Axes of the slice: x: 4, y: 4 (y_hi: 2, y_lo: 2; y = y_hi * 2 + y_lo), z: 8, core: 2. Of those that a mesh axis runs over, the one named last changes fastest.
Arguments:
- fields: float32 [5, 64, 64, 8, 512], P(None, None, 'az', 'rad', 'ht'), may hold values from -6 to 6
- inverse_blocks: bfloat16 [64, 64, 64, 8, 512], P(None, None, 'az', 'rad', 'ht'), may hold values from -0.75 to 0.75
- stiffness: bfloat16 [3, 64, 64], replicated, may hold values from -0.75 to 0.75
- wind_field: bfloat16 [3, 64, 64, 8, 512], P(None, None, 'az', 'rad', 'ht'), may hold values from -3 to 3
- face_decay: float32 [16, 64, 8, 512], P(None, 'az', 'rad', 'ht'), may hold values from 0 to 1
- wall_kind: int32 [2, 64, 512], P(None, 'az', 'ht'), may hold values from 0 to 2
Outputs:
- advanced: float32 [5, 64, 64, 8, 512], P(None, None, 'az', 'rad', 'ht')
The draws below stay inside these ranges and needn't reach their ends.
All inputs are finite; a program needn't handle non-finite values.
Results may differ from the reference program's by a relative error of at most 0.0034.
Values sent between devices are 32-bit elements; how exact they have to be, the bound alone decides.
A program may use at most 128 MiB of HBM per device.

```python
import jax
import jax.numpy as jnp
from jax import lax

FIELDS = 5
NODES = 64
AZIMUTH_COUNT = 64
NRE = 8
NHE = 512


def draw_face_decay(key, part):
    parallel_flows = jax.random.split(key, 6)
    extent = (16, AZIMUTH_COUNT, NRE, NHE)
    lasting_share = 0.5
    pulse_low = 0.22
    pulse_high = 0.6
    persistent_part = jax.random.uniform(parallel_flows[0], (16, 1, NRE, NHE)) < lasting_share
    gradual_decay_rate = jnp.exp(jax.random.uniform(parallel_flows[1], (16, 1, NRE, NHE), minval=jnp.log(0.2), maxval=0.0)) / AZIMUTH_COUNT
    quick_decay_rate = jnp.exp(-jax.random.uniform(parallel_flows[2], (16, 1, NRE, NHE), minval=jnp.log(20.0), maxval=jnp.log(50.0)))
    dispersion_width = jax.random.uniform(parallel_flows[3], extent, minval=0.5, maxval=1.5)
    pulse_places = jax.random.uniform(parallel_flows[4], extent) < 2.5 / AZIMUTH_COUNT
    pulse_sizes = jax.random.uniform(parallel_flows[5], extent, minval=pulse_low, maxval=pulse_high)
    pulse_events = jnp.where(pulse_places, pulse_sizes, 0.0)
    return (jnp.where(persistent_part, gradual_decay_rate, quick_decay_rate) * dispersion_width + pulse_events).astype(jnp.float32)


def with_ends(array, key, low, largest):
    longest = array.shape.index(max(array.shape))
    spots = []
    for shift in (0, 1):
        where = [jax.random.randint(jax.random.fold_in(key, axis), (), 0, length) for axis, length in enumerate(array.shape)]
        where[longest] = (where[longest] + shift) % array.shape[longest]
        spots.append(tuple(where))
    return array.at[spots[0]].set(low).at[spots[1]].set(largest)


def shard_levels(rng, dims, cuts, smallest, high):
    loudness = 1.0
    for axis_at, shards_of in cuts:
        heights = jax.random.uniform(jax.random.fold_in(jax.random.fold_in(rng, 6), axis_at), (shards_of,), jnp.float32, smallest / len(cuts), high / len(cuts))
        loudness = loudness * jnp.repeat(jnp.exp(heights), dims[axis_at] // shards_of).reshape((-1,) + (1,) * (len(dims) - 1 - axis_at))
    return loudness


def noise(key, dims, width, bound, cuts=(), held_as=jnp.bfloat16):
    result = width * jax.random.normal(key, dims, jnp.float32)
    if cuts:
        result = result * shard_levels(key, dims, cuts, -0.22, 0.18)
    return jnp.clip(result, -bound, bound).astype(held_as)


def setup_inputs(seed: int = 0) -> dict:
    key_list = jax.random.split(jax.random.key(seed), 7)
    fields = noise(key_list[0], (FIELDS, NODES, AZIMUTH_COUNT, NRE, NHE), 1.0, 6.0, ((2, 64), (3, 2), (4, 2)), jnp.float32)
    inverse_blocks = noise(key_list[1], (NODES, NODES, AZIMUTH_COUNT, NRE, NHE), 64 ** -0.5, 0.75, ((2, 64), (3, 2), (4, 2)))
    stiffness = noise(key_list[2], (3, NODES, NODES), 64 ** -0.5, 0.75)
    wind_field = noise(key_list[3], (3, NODES, AZIMUTH_COUNT, NRE, NHE), 0.5, 3.0, ((2, 64), (3, 2), (4, 2)))
    face_decay = draw_face_decay(jax.random.fold_in(key_list[6], 71), 0)
    wall_kind = with_ends(jax.random.randint(key_list[5], (2, AZIMUTH_COUNT, NHE), 0, 3), jax.random.fold_in(key_list[5], 1), 0, 2).astype(jnp.int32)
    return dict(fields=fields, inverse_blocks=inverse_blocks, stiffness=stiffness, wind_field=wind_field, face_decay=face_decay, wall_kind=wall_kind)


PENALTY = 2.0
TIME_STEP = 0.2


def wall_factor(wall_code):
    field_index = jnp.arange(5).reshape(5, 1, 1, 1, 1, 1)
    wall_type = wall_code[None, None, None, :, None, :]
    return jnp.where(wall_type == 1, 0.0, jnp.where((wall_type == 0) & (field_index == 2), -1.0, 1.0))


def reference(fields, inverse_blocks, stiffness, wind_field, face_decay, wall_kind):
    count_az, count_rad, count_ht = fields.shape[2], fields.shape[3], fields.shape[4]
    coarse = fields.astype(jnp.bfloat16).astype(jnp.float32)
    tendency = jnp.zeros(fields.shape, jnp.float32)
    for direction in range(3):
        slopes = jnp.einsum('mn,fnarh->fmarh', stiffness[direction].astype(jnp.float32), coarse)
        tendency = tendency - wind_field[direction].astype(jnp.float32)[None] * slopes
    shaped = fields.reshape(5, 4, 4, 4, count_az, count_rad, count_ht)
    growth = tendency.reshape(5, 4, 4, 4, count_az, count_rad, count_ht)
    left_face = shaped[:, :, :, 0]
    right_face = shaped[:, :, :, 3]
    growth = growth.at[:, :, :, 0].add(PENALTY * (jnp.roll(right_face, 1, axis=3) - left_face))
    growth = growth.at[:, :, :, 3].add(PENALTY * (jnp.roll(left_face, -1, axis=3) - right_face))
    inner_face = shaped[:, :, 0]
    outer_face = shaped[:, :, 3]
    inner_ghost = jnp.concatenate([wall_factor(wall_kind[0]) * inner_face[:, :, :, :, :1], outer_face[:, :, :, :, :-1]], axis=4)
    outer_ghost = jnp.concatenate([inner_face[:, :, :, :, 1:], wall_factor(wall_kind[1]) * outer_face[:, :, :, :, -1:]], axis=4)
    growth = growth.at[:, :, 0].add(PENALTY * (inner_ghost - inner_face))
    growth = growth.at[:, :, 3].add(PENALTY * (outer_ghost - outer_face))
    lower_face = shaped[:, 0]
    upper_face = shaped[:, 3]
    zero_row = jnp.zeros_like(lower_face[..., :1])
    lower_ghost = jnp.concatenate([zero_row, upper_face[..., :-1]], axis=5)
    upper_ghost = jnp.concatenate([lower_face[..., 1:], zero_row], axis=5)
    growth = growth.at[:, 0].add(PENALTY * (lower_ghost - lower_face))
    growth = growth.at[:, 3].add(PENALTY * (upper_ghost - upper_face))
    sectioned = fields + TIME_STEP * growth.reshape(fields.shape)

    pressure_rhs = sectioned[4].astype(jnp.bfloat16)
    decays = jnp.exp(-face_decay)
    shares = -jnp.expm1(-face_decay)
    positions = jnp.arange(count_az, dtype=jnp.int32)

    def first_pass(carried, position):
        blocks_here = lax.dynamic_index_in_dim(inverse_blocks, position, 2, keepdims=False).astype(jnp.float32)
        column = lax.dynamic_index_in_dim(pressure_rhs, position, 1, keepdims=False).astype(jnp.float32)
        solved_here = jnp.einsum('mnrh,nrh->mrh', blocks_here, column)
        exit_here = solved_here.reshape(4, 4, 4, count_rad, count_ht)[:, :, 3].reshape(16, count_rad, count_ht)
        rate_here = lax.dynamic_index_in_dim(decays, position, 1, keepdims=False)
        share_here = lax.dynamic_index_in_dim(shares, position, 1, keepdims=False)
        product, offset = carried
        return (product * rate_here, rate_here * offset + share_here * exit_here), solved_here

    unity = jnp.ones((16, count_rad, count_ht), jnp.float32)
    nothing = jnp.zeros((16, count_rad, count_ht), jnp.float32)
    (product, offset), solved = lax.scan(first_pass, (unity, nothing), positions)
    loop_start = offset / (1.0 - product)

    def second_pass(previous, position):
        blocks_here = lax.dynamic_index_in_dim(inverse_blocks, position, 2, keepdims=False).astype(jnp.float32)
        solved_here = solved[position]
        exit_here = solved_here.reshape(4, 4, 4, count_rad, count_ht)[:, :, 3].reshape(16, count_rad, count_ht)
        rate_here = lax.dynamic_index_in_dim(decays, position, 1, keepdims=False)
        share_here = lax.dynamic_index_in_dim(shares, position, 1, keepdims=False)
        left_columns = blocks_here.reshape(64, 4, 4, 4, count_rad, count_ht)[:, :, :, 0].reshape(64, 16, count_rad, count_ht)
        rounded = lax.optimization_barrier(previous.astype(jnp.bfloat16)).astype(jnp.float32)
        pressure = solved_here + jnp.einsum('mcrh,crh->mrh', left_columns, rounded)
        following = rate_here * previous + share_here * exit_here
        return following, pressure

    unused, pressures = lax.scan(second_pass, loop_start, positions)
    return sectioned.at[4].set(jnp.moveaxis(pressures, 0, 1))
```

```python
import jax
import jax.numpy as jnp
from jax import lax
from jax.experimental import pallas as pl
from jax.experimental.pallas import tpu as pltpu
from jax.sharding import PartitionSpec as P

MESH = pl.DeviceIdType.MESH
F32 = jnp.float32
BF16 = jnp.bfloat16
FIELDS = 5
PRESSURE = 4
PENALTY = 2.0
TIME_STEP = 0.2
GAIN = PENALTY * TIME_STEP
GROUP = 8
EXPM1_TERMS = 11
IB_PARTS = 4


def tiles(cells):
    lead = cells.shape[:-3]
    n = len(lead)
    cells = cells.reshape(lead + (4, 2, 128))
    cells = cells.transpose(tuple(range(n)) + (n + 1, n, n + 2))
    return cells.reshape(lead + (8, 128))


def untiles(cells):
    lead = cells.shape[:-2]
    n = len(lead)
    cells = cells.reshape(lead + (2, 4, 128))
    cells = cells.transpose(tuple(range(n)) + (n + 1, n, n + 2))
    return cells.reshape(lead + (1, 4, 256))


def lost_share(decay):
    total = jnp.full_like(decay, 1.0)
    for term in range(EXPM1_TERMS, 1, -1):
        total = 1.0 - decay * total * (1.0 / term)
    return decay * total


def kernel(
    fields, blocks, stiff, wind, decay, walls, out,
    fv, ibv, stv, wv, dv, kv, acc, sl, rv, sol,
    hl, hr, rr, hp, hq, dbuf, pbuf, obuf, zbuf, ibuf, rates, share, off, pblk, oblk, wbuf, into,
    local_sem, out_sem, send_sem, recv_sem,
):
    az = lax.axis_index("az")
    rad = lax.axis_index("rad")
    ht = lax.axis_index("ht")
    count = 64
    g = lax.rem(az, GROUP)
    z = lax.div(az, GROUP)
    first = az - g
    right = {"az": lax.rem(az + 1, count)}
    left = {"az": lax.rem(az + count - 1, count)}
    other_rad = {"rad": 1 - rad}
    other_ht = {"ht": 1 - ht}
    mates = [{"az": first + lax.rem(g + k, GROUP)} for k in range(1, GROUP)]
    peers = [{"az": lax.rem(az + GROUP * k, count)} for k in range(1, 8)]

    loads = {}

    def load(name, src, dst):
        copy = pltpu.make_async_copy(src, dst, local_sem.at[len(loads)])
        loads[name] = copy
        copy.start()

    load("p", fields.at[PRESSURE], fv.at[PRESSURE])
    load("st", stiff, stv)
    load("w", wind, wv)
    load("d", decay, dv)
    load("k", walls, kv)
    rows = 64 // IB_PARTS
    for part in range(IB_PARTS):
        load("ib%d" % part, blocks.at[pl.ds(part * rows, rows)], ibv.at[pl.ds(part * rows, rows)])
    load("f", fields.at[pl.ds(0, 4)], fv.at[pl.ds(0, 4)])

    barrier = pltpu.get_barrier_semaphore()
    partners = mates + peers + [right, left, other_rad, other_ht]
    for partner in partners:
        pl.semaphore_signal(barrier, inc=1, device_id=partner, device_id_type=MESH)
    pl.semaphore_wait(barrier, len(partners))

    sent = []

    def send(src, dst, partner):
        slot = len(sent)
        copy = pltpu.make_async_remote_copy(
            src_ref=src, dst_ref=dst, send_sem=send_sem.at[slot], recv_sem=recv_sem.at[slot],
            device_id=partner, device_id_type=MESH,
        )
        sent.append(copy)
        copy.start()
        return copy

    def az_halo(f):
        to_right = send(nodes(fields, f).at[:, 3], hl.at[f], right)
        to_left = send(nodes(fields, f).at[:, 0], hr.at[f], left)
        return to_right, to_left

    def nodes(ref, f):
        return ref.at[f].reshape(16, 4, 8, 128)

    halo = {}
    halo[PRESSURE] = az_halo(PRESSURE)
    rad_j = 3 * (1 - rad)
    rad_p = send(fields.at[PRESSURE].reshape(4, 4, 4, 8, 128).at[:, rad_j], rr.at[PRESSURE], other_rad)
    rates_in = []
    for k in range(1, GROUP):
        mate = lax.rem(g + k, GROUP)
        rates_in.append(send(decay.at[pl.ds(2 * mate, 2)], dbuf.at[g], mates[k - 1]))
    halo[0] = az_halo(0)
    rad_f = send(fields.at[pl.ds(0, 4)].reshape(4, 4, 4, 4, 8, 128).at[:, :, rad_j], rr.at[pl.ds(0, 4)], other_rad)

    row = lax.broadcasted_iota(jnp.int32, (8, 128), 0)
    lane = lax.broadcasted_iota(jnp.int32, (8, 128), 1)
    radius = lax.rem(row, 4)

    ht_l = 3 * (1 - ht)

    def pack(f):
        packed = jnp.zeros((8, 128), F32)
        for q in range(16):
            packed = jnp.where(lane == q + ht, pltpu.roll(fv[f, 16 * ht_l + q], q + 1, 1), packed)
        hp[f] = packed

    loads["p"].wait()
    pack(PRESSURE)
    ht_p = send(hp.at[PRESSURE], hq.at[PRESSURE], other_ht)

    def slopes(f):
        columns = jnp.concatenate(
            [fv.at[f].reshape(512, 128)[pl.ds(s, 64, stride=8), :].astype(BF16) for s in range(8)], axis=1
        )
        product = jnp.dot(stv[...], columns, preferred_element_type=F32)
        for s in range(8):
            sl[pl.ds(s, 192, stride=8), :] = product[:, 128 * s : 128 * (s + 1)]

        def node(n, carry):
            total = None
            for d in range(3):
                term = wv[d, n].astype(F32) * sl[pl.ds(pl.multiple_of((64 * d + n) * 8, 8), 8), :]
                total = term if total is None else total + term
            acc[f, n] = fv[f, n] - TIME_STEP * total
            return carry

        lax.fori_loop(0, 64, node, 0, unroll=8)

    def wall_codes(side):
        low = jnp.broadcast_to(kv[2 * side : 2 * side + 1, :], (8, 128))
        high = jnp.broadcast_to(kv[2 * side + 1 : 2 * side + 2, :], (8, 128))
        return jnp.where(row < 4, low, high)

    loads["st"].wait()
    loads["w"].wait()
    loads["k"].wait()
    codes = [wall_codes(0), wall_codes(1)]
    inner_row = radius == 0
    outer_row = radius == 3
    low_rows = row < 4
    is_rad0 = (row * 0 + rad) == 0
    is_ht0 = (row * 0 + ht) == 0

    def side_faces(f, is_field_2):
        factors = [
            jnp.where(code == 1, 0.0, jnp.where(code == 0, 1.0 - 2.0 * is_field_2, 1.0)) for code in codes
        ]
        for l in range(4):
            for i in range(4):
                n_in, n_out = 16 * l + i, 16 * l + 12 + i
                own_in, own_out = fv[f, n_in], fv[f, n_out]
                beside = rr[f, l, i]
                edge_in = jnp.where(is_rad0, factors[0] * own_in, pltpu.roll(beside, 5, 0))
                edge_out = jnp.where(is_rad0, pltpu.roll(beside, 3, 0), factors[1] * own_out)
                ghost_in = jnp.where(inner_row, edge_in, pltpu.roll(own_out, 1, 0))
                ghost_out = jnp.where(outer_row, edge_out, pltpu.roll(own_in, 7, 0))
                acc[f, n_in] += GAIN * (ghost_in - own_in)
                acc[f, n_out] += GAIN * (ghost_out - own_out)
        packed = hq[f]
        from_low = jnp.where(is_ht0, 0.0, packed)
        from_high = jnp.where(is_ht0, packed, 0.0)
        for q in range(16):
            own_low, own_high = fv[f, q], fv[f, 48 + q]
            turned = pltpu.roll(jnp.where(low_rows, own_high, pltpu.roll(from_low, 127 - q, 1)), 4, 0)
            ghost_low = pltpu.roll(jnp.where(lane == 127, turned, own_high), 1, 1)
            turned = pltpu.roll(jnp.where(low_rows, pltpu.roll(from_high, 127 - q, 1), own_low), 4, 0)
            ghost_high = pltpu.roll(jnp.where(lane == 0, turned, own_low), 127, 1)
            acc[f, q] += GAIN * (ghost_low - own_low)
            acc[f, 48 + q] += GAIN * (ghost_high - own_high)

    def az_faces(f):
        for q in range(16):
            acc[f, 4 * q] += GAIN * (hl[f, q] - fv[f, 4 * q])
            acc[f, 4 * q + 3] += GAIN * (hr[f, q] - fv[f, 4 * q + 3])

    slopes(PRESSURE)
    loads["f"].wait()
    for f in range(4):
        pack(f)
    ht_f = send(hp.at[pl.ds(0, 4)], hq.at[pl.ds(0, 4)], other_ht)
    loads["d"].wait()

    def own_share(c, carry):
        share[c] = lost_share(dv[c])
        return carry

    lax.fori_loop(0, 16, own_share, 0, unroll=4)
    rad_p.wait_recv()
    ht_p.wait_recv()
    side_faces(PRESSURE, 0.0)

    for copy in rates_in:
        copy.wait_recv()
    dbuf[g] = dv[pl.ds(2 * g, 2)]
    passed = None
    for t in range(GROUP):
        rate = jnp.exp(-dbuf[t])
        rates[t] = rate
        passed = rate if passed is None else passed * rate
    pblk[...] = passed
    pbuf[z] = passed
    blocks_in = [send(pblk, pbuf.at[z], peer) for peer in peers]

    for copy in halo[PRESSURE]:
        copy.wait_recv()
    az_faces(PRESSURE)

    def rounded(n, carry):
        rv[n] = acc[PRESSURE, n].astype(BF16).astype(F32)
        return carry

    lax.fori_loop(0, 64, rounded, 0, unroll=8)
    for part in range(IB_PARTS):
        loads["ib%d" % part].wait()

    def product(m):
        sums = [None] * 4
        for n in range(64):
            term = ibv[m, n].astype(F32) * rv[n]
            sums[n % 4] = term if sums[n % 4] is None else sums[n % 4] + term
        return (sums[0] + sums[1]) + (sums[2] + sums[3])

    def exit_row(c, carry):
        solved = product(4 * c + 3)
        sol[4 * c + 3] = solved
        off[c] = share[c] * solved
        return carry

    lax.fori_loop(0, 16, exit_row, 0)
    offsets_in = []
    for k in range(1, GROUP):
        mate = lax.rem(g + k, GROUP)
        offsets_in.append(send(off.at[pl.ds(2 * mate, 2)], obuf.at[g], mates[k - 1]))
    halo[1] = az_halo(1)

    def other_rows(c, carry):
        for i in range(3):
            sol[4 * c + i] = product(4 * c + i)
        return carry

    lax.fori_loop(0, 16, other_rows, 0)

    for copy in blocks_in:
        copy.wait_recv()
    whole = pbuf[0]
    for t in range(1, 8):
        whole = whole * pbuf[t]
    weight = 1.0 / (1.0 - whole)
    for k in range(1, 9):
        wbuf[k - 1] = weight
        if k < 8:
            weight = weight * pbuf[lax.rem(z + 8 - k, 8)]

    for copy in offsets_in:
        copy.wait_recv()
    obuf[g] = off[pl.ds(2 * g, 2)]
    state = jnp.zeros((2, 8, 128), F32)
    passed = jnp.ones((2, 8, 128), F32)
    for t in range(GROUP):
        into[t] = state
        state = rates[t] * state + obuf[t]
    oblk[...] = state
    zbuf[z] = state
    totals_in = [send(oblk, zbuf.at[z], peer) for peer in peers]

    slopes(0)
    for copy in totals_in:
        copy.wait_recv()
    start = jnp.zeros((2, 8, 128), F32)
    for k in range(1, 9):
        start = start + wbuf[k - 1] * zbuf[lax.rem(z + 8 - k, 8)]
    for t in range(GROUP):
        into[t] = into[t] + passed * start
        passed = passed * rates[t]
    ibuf[pl.ds(2 * g, 2)] = into[g]
    carried_in = []
    for k in range(1, GROUP):
        mate = lax.rem(g + k, GROUP)
        carried_in.append(send(into.at[mate], ibuf.at[pl.ds(2 * g, 2)], mates[k - 1]))
    halo[2] = az_halo(2)
    halo[3] = az_halo(3)

    for f in range(1, 4):
        slopes(f)
    rad_f.wait_recv()
    ht_f.wait_recv()

    def sides(f, carry):
        side_faces(f, jnp.where(f == 2, 1.0, 0.0))
        return carry

    lax.fori_loop(0, 4, sides, 0)

    stores = []

    def finish(f):
        copy = pltpu.make_async_copy(acc.at[f], out.at[f], out_sem.at[f])
        copy.start()
        stores.append(copy)

    def finish_az(f):
        for copy in halo[f]:
            copy.wait_recv()
        az_faces(f)
        finish(f)

    finish_az(0)
    finish_az(1)

    for copy in carried_in:
        copy.wait_recv()

    def round_into(c, carry):
        rv[c] = ibuf[c].astype(BF16).astype(F32)
        return carry

    lax.fori_loop(0, 16, round_into, 0, unroll=8)

    def corrected(m, carry):
        sums = [sol[m], None]
        for c in range(16):
            term = ibv[m, 4 * c].astype(F32) * rv[c]
            sums[c % 2] = term if sums[c % 2] is None else sums[c % 2] + term
        acc[PRESSURE, m] = sums[0] + sums[1]
        return carry

    lax.fori_loop(0, 64, corrected, 0, unroll=2)
    finish(PRESSURE)
    finish_az(2)
    finish_az(3)
    for copy in sent:
        copy.wait_send()
    for copy in stores:
        copy.wait()


def per_device(fields, inverse_blocks, stiffness, wind_field, face_decay, wall_kind):
    hbm = pl.BlockSpec(memory_space=pltpu.HBM)
    vmem = pltpu.VMEM
    tile = (8, 128)
    lines = (GROUP, 2) + tile
    advanced = pl.pallas_call(
        kernel,
        in_specs=[hbm] * 6,
        out_specs=hbm,
        out_shape=jax.ShapeDtypeStruct((FIELDS, 64) + tile, F32),
        scratch_shapes=[
            vmem((FIELDS, 64) + tile, F32),
            vmem((64, 64) + tile, BF16),
            vmem((192, 64), BF16),
            vmem((3, 64) + tile, BF16),
            vmem((16,) + tile, F32),
            vmem((4, 128), jnp.int32),
            vmem((FIELDS, 64) + tile, F32),
            vmem((1536, 128), F32),
            vmem((64,) + tile, F32),
            vmem((64,) + tile, F32),
            vmem((FIELDS, 16) + tile, F32),
            vmem((FIELDS, 16) + tile, F32),
            vmem((FIELDS, 4, 4) + tile, F32),
            vmem((FIELDS,) + tile, F32),
            vmem((FIELDS,) + tile, F32),
            vmem(lines, F32),
            vmem(lines, F32),
            vmem(lines, F32),
            vmem(lines, F32),
            vmem((16,) + tile, F32),
            vmem(lines, F32),
            vmem((16,) + tile, F32),
            vmem((16,) + tile, F32),
            vmem((2,) + tile, F32),
            vmem((2,) + tile, F32),
            vmem(lines, F32),
            vmem(lines, F32),
            pltpu.SemaphoreType.DMA((6 + IB_PARTS,)),
            pltpu.SemaphoreType.DMA((FIELDS,)),
            pltpu.SemaphoreType.DMA((49,)),
            pltpu.SemaphoreType.DMA((49,)),
        ],
        compiler_params=pltpu.CompilerParams(
            collective_id=0, has_side_effects=True, vmem_limit_bytes=48 << 20
        ),
        name="section",
    )(
        tiles(fields),
        tiles(inverse_blocks),
        stiffness.reshape(192, 64),
        tiles(wind_field),
        tiles(face_decay),
        wall_kind.reshape(4, 128),
    )
    return untiles(advanced)


def solution(mesh):
    placed = (
        P(None, None, "az", "rad", "ht"),
        P(None, None, "az", "rad", "ht"),
        P(),
        P(None, None, "az", "rad", "ht"),
        P(None, "az", "rad", "ht"),
        P(None, "az", "ht"),
    )
    return jax.shard_map(
        per_device,
        mesh=mesh,
        in_specs=placed,
        out_specs=P(None, None, "az", "rad", "ht"),
        check_vma=False,
    )
```

```python
import jax
import jax.numpy as jnp
from jax import lax
from jax.experimental import pallas as pl
from jax.experimental.pallas import tpu as pltpu
from jax.sharding import PartitionSpec as P

MESH = pl.DeviceIdType.MESH
F32 = jnp.float32
BF16 = jnp.bfloat16
FIELDS = 5
PRESSURE = 4
PENALTY = 2.0
TIME_STEP = 0.2
GAIN = PENALTY * TIME_STEP
GROUP = 8
EXPM1_TERMS = 11
IB_PARTS = 4


def tiles(cells):
    lead = cells.shape[:-3]
    n = len(lead)
    cells = cells.reshape(lead + (4, 2, 128))
    cells = cells.transpose(tuple(range(n)) + (n + 1, n, n + 2))
    return cells.reshape(lead + (8, 128))


def untiles(cells):
    lead = cells.shape[:-2]
    n = len(lead)
    cells = cells.reshape(lead + (2, 4, 128))
    cells = cells.transpose(tuple(range(n)) + (n + 1, n, n + 2))
    return cells.reshape(lead + (1, 4, 256))


def lost_share(decay):
    total = jnp.full_like(decay, 1.0)
    for term in range(EXPM1_TERMS, 1, -1):
        total = 1.0 - decay * total * (1.0 / term)
    return decay * total


def kernel(
    fields, blocks, stiff, wind, decay, walls, acc,
    fv, ibv, stv, wv, dv, kv, sl, rv, sol,
    hl, hr, rr, hp, hq, dbuf, pbuf, obuf, zbuf, ibuf, rates, share, off, pblk, oblk, wbuf, into,
    local_sem, send_sem, recv_sem,
):
    az = lax.axis_index("az")
    rad = lax.axis_index("rad")
    ht = lax.axis_index("ht")
    count = 64
    g = lax.rem(az, GROUP)
    z = lax.div(az, GROUP)
    first = az - g
    right = {"az": lax.rem(az + 1, count)}
    left = {"az": lax.rem(az + count - 1, count)}
    other_rad = {"rad": 1 - rad}
    other_ht = {"ht": 1 - ht}
    mates = [{"az": first + lax.rem(g + k, GROUP)} for k in range(1, GROUP)]
    peers = [{"az": lax.rem(az + GROUP * k, count)} for k in range(1, 8)]

    loads = {}

    def load(name, src, dst):
        copy = pltpu.make_async_copy(src, dst, local_sem.at[len(loads)])
        loads[name] = copy
        copy.start()

    load("p", fields.at[PRESSURE], fv.at[PRESSURE])
    load("st", stiff, stv)
    load("w", wind, wv)
    load("d", decay, dv)
    load("k", walls, kv)
    load("f", fields.at[pl.ds(0, 4)], fv.at[pl.ds(0, 4)])
    rows = 64 // IB_PARTS
    for part in range(IB_PARTS):
        load("ib%d" % part, blocks.at[pl.ds(part * rows, rows)], ibv.at[pl.ds(part * rows, rows)])

    barrier = pltpu.get_barrier_semaphore()
    partners = mates + peers + [right, left, other_rad, other_ht]
    for partner in partners:
        pl.semaphore_signal(barrier, inc=1, device_id=partner, device_id_type=MESH)
    pl.semaphore_wait(barrier, len(partners))

    sent = []

    def send(src, dst, partner):
        slot = len(sent)
        copy = pltpu.make_async_remote_copy(
            src_ref=src, dst_ref=dst, send_sem=send_sem.at[slot], recv_sem=recv_sem.at[slot],
            device_id=partner, device_id_type=MESH,
        )
        sent.append(copy)
        copy.start()
        return copy

    def nodes(ref, f):
        return ref.at[f].reshape(16, 4, 8, 128)

    def to_right(f):
        return send(nodes(fields, f).at[:, 3], hl.at[f], right)

    def to_left(f):
        return send(nodes(fields, f).at[:, 0], hr.at[f], left)

    def az_halo(f):
        return to_right(f), to_left(f)

    row = lax.broadcasted_iota(jnp.int32, (8, 128), 0)
    lane = lax.broadcasted_iota(jnp.int32, (8, 128), 1)
    radius = lax.rem(row, 4)

    ht_l = 3 * (1 - ht)

    def pack(f):
        packed = jnp.zeros((8, 128), F32)
        for q in range(16):
            packed = jnp.where(lane == q + ht, pltpu.roll(fv[f, 16 * ht_l + q], q + 1, 1), packed)
        hp[f] = packed

    halo = {}
    rad_j = 3 * (1 - rad)
    rad_p = send(fields.at[PRESSURE].reshape(4, 4, 4, 8, 128).at[:, rad_j], rr.at[PRESSURE], other_rad)
    halo_right = to_right(PRESSURE)
    loads["p"].wait()
    pack(PRESSURE)
    ht_p = send(hp.at[PRESSURE], hq.at[PRESSURE], other_ht)
    halo[PRESSURE] = halo_right, to_left(PRESSURE)
    rates_in = []
    for k in range(1, GROUP):
        mate = lax.rem(g + k, GROUP)
        rates_in.append(send(decay.at[pl.ds(2 * mate, 2)], dbuf.at[g], mates[k - 1]))
    rad_f = send(fields.at[pl.ds(0, 4)].reshape(4, 4, 4, 4, 8, 128).at[:, :, rad_j], rr.at[pl.ds(0, 4)], other_rad)

    def slopes(f):
        columns = jnp.concatenate(
            [fv.at[f].reshape(512, 128)[pl.ds(s, 64, stride=8), :].astype(BF16) for s in range(8)], axis=1
        )
        product = jnp.dot(stv[...], columns, preferred_element_type=F32)
        for s in range(8):
            sl[pl.ds(s, 192, stride=8), :] = product[:, 128 * s : 128 * (s + 1)]

        def node(n, carry):
            total = None
            for d in range(3):
                term = wv[d, n].astype(F32) * sl[pl.ds(pl.multiple_of((64 * d + n) * 8, 8), 8), :]
                total = term if total is None else total + term
            acc[f, n] = fv[f, n] - TIME_STEP * total
            return carry

        lax.fori_loop(0, 64, node, 0, unroll=8)

    def wall_codes(side):
        low = jnp.broadcast_to(kv[2 * side : 2 * side + 1, :], (8, 128))
        high = jnp.broadcast_to(kv[2 * side + 1 : 2 * side + 2, :], (8, 128))
        return jnp.where(row < 4, low, high)

    loads["st"].wait()
    loads["w"].wait()
    loads["k"].wait()
    codes = [wall_codes(0), wall_codes(1)]
    inner_row = radius == 0
    outer_row = radius == 3
    low_rows = row < 4
    is_rad0 = (row * 0 + rad) == 0
    is_ht0 = (row * 0 + ht) == 0

    def side_faces(f, is_field_2):
        factors = [
            jnp.where(code == 1, 0.0, jnp.where(code == 0, 1.0 - 2.0 * is_field_2, 1.0)) for code in codes
        ]
        for l in range(4):
            for i in range(4):
                n_in, n_out = 16 * l + i, 16 * l + 12 + i
                own_in, own_out = fv[f, n_in], fv[f, n_out]
                beside = rr[f, l, i]
                edge_in = jnp.where(is_rad0, factors[0] * own_in, pltpu.roll(beside, 5, 0))
                edge_out = jnp.where(is_rad0, pltpu.roll(beside, 3, 0), factors[1] * own_out)
                ghost_in = jnp.where(inner_row, edge_in, pltpu.roll(own_out, 1, 0))
                ghost_out = jnp.where(outer_row, edge_out, pltpu.roll(own_in, 7, 0))
                acc[f, n_in] += GAIN * (ghost_in - own_in)
                acc[f, n_out] += GAIN * (ghost_out - own_out)
        packed = hq[f]
        from_low = jnp.where(is_ht0, 0.0, packed)
        from_high = jnp.where(is_ht0, packed, 0.0)
        for q in range(16):
            own_low, own_high = fv[f, q], fv[f, 48 + q]
            turned = pltpu.roll(jnp.where(low_rows, own_high, pltpu.roll(from_low, 127 - q, 1)), 4, 0)
            ghost_low = pltpu.roll(jnp.where(lane == 127, turned, own_high), 1, 1)
            turned = pltpu.roll(jnp.where(low_rows, pltpu.roll(from_high, 127 - q, 1), own_low), 4, 0)
            ghost_high = pltpu.roll(jnp.where(lane == 0, turned, own_low), 127, 1)
            acc[f, q] += GAIN * (ghost_low - own_low)
            acc[f, 48 + q] += GAIN * (ghost_high - own_high)

    def az_faces(f):
        for q in range(16):
            acc[f, 4 * q] += GAIN * (hl[f, q] - fv[f, 4 * q])
            acc[f, 4 * q + 3] += GAIN * (hr[f, q] - fv[f, 4 * q + 3])

    slopes(PRESSURE)
    loads["f"].wait()
    for f in range(4):
        pack(f)
    ht_f = send(hp.at[pl.ds(0, 4)], hq.at[pl.ds(0, 4)], other_ht)
    loads["d"].wait()

    def own_share(c, carry):
        share[c] = lost_share(dv[c])
        return carry

    lax.fori_loop(0, 16, own_share, 0, unroll=4)
    rad_p.wait_recv()
    ht_p.wait_recv()
    side_faces(PRESSURE, 0.0)

    for copy in halo[PRESSURE]:
        copy.wait_recv()
    az_faces(PRESSURE)

    def rounded(n, carry):
        rv[n] = acc[PRESSURE, n].astype(BF16).astype(F32)
        return carry

    lax.fori_loop(0, 64, rounded, 0, unroll=8)
    for part in range(IB_PARTS):
        loads["ib%d" % part].wait()

    def product(m):
        sums = [None] * 4
        for n in range(64):
            term = ibv[m, n].astype(F32) * rv[n]
            sums[n % 4] = term if sums[n % 4] is None else sums[n % 4] + term
        return (sums[0] + sums[1]) + (sums[2] + sums[3])

    def exit_row(c, carry):
        solved = product(4 * c + 3)
        sol[4 * c + 3] = solved
        off[c] = share[c] * solved
        return carry

    lax.fori_loop(0, 16, exit_row, 0)
    offsets_in = []
    for k in range(1, GROUP):
        mate = lax.rem(g + k, GROUP)
        offsets_in.append(send(off.at[pl.ds(2 * mate, 2)], obuf.at[g], mates[k - 1]))

    for copy in rates_in:
        copy.wait_recv()
    dbuf[g] = dv[pl.ds(2 * g, 2)]
    passed = None
    for t in range(GROUP):
        rate = jnp.exp(-dbuf[t])
        rates[t] = rate
        passed = rate if passed is None else passed * rate
    pblk[...] = passed
    pbuf[z] = passed
    blocks_in = [send(pblk, pbuf.at[z], peer) for peer in peers]

    halo[0] = az_halo(0)

    def other_rows(c, carry):
        for i in range(3):
            sol[4 * c + i] = product(4 * c + i)
        return carry

    lax.fori_loop(0, 16, other_rows, 0)

    for copy in offsets_in:
        copy.wait_recv()
    obuf[g] = off[pl.ds(2 * g, 2)]
    state = jnp.zeros((2, 8, 128), F32)
    passed = jnp.ones((2, 8, 128), F32)
    for t in range(GROUP):
        into[t] = state
        state = rates[t] * state + obuf[t]
    oblk[...] = state
    zbuf[z] = state
    totals_in = [send(oblk, zbuf.at[z], peer) for peer in peers]

    halo[1] = az_halo(1)
    halo[2] = az_halo(2)
    slopes(0)
    for copy in blocks_in:
        copy.wait_recv()
    whole = pbuf[0]
    for t in range(1, 8):
        whole = whole * pbuf[t]
    weight = 1.0 / (1.0 - whole)
    for k in range(1, 9):
        wbuf[k - 1] = weight
        if k < 8:
            weight = weight * pbuf[lax.rem(z + 8 - k, 8)]

    for copy in totals_in:
        copy.wait_recv()
    start = jnp.zeros((2, 8, 128), F32)
    for k in range(1, 9):
        start = start + wbuf[k - 1] * zbuf[lax.rem(z + 8 - k, 8)]
    for t in range(GROUP):
        into[t] = into[t] + passed * start
        passed = passed * rates[t]
    ibuf[pl.ds(2 * g, 2)] = into[g]
    carried_in = []
    for k in range(1, GROUP):
        mate = lax.rem(g + k, GROUP)
        carried_in.append(send(into.at[mate], ibuf.at[pl.ds(2 * g, 2)], mates[k - 1]))

    halo[3] = az_halo(3)
    for f in range(1, 4):
        slopes(f)
    rad_f.wait_recv()
    ht_f.wait_recv()

    def sides(f, carry):
        side_faces(f, jnp.where(f == 2, 1.0, 0.0))
        return carry

    lax.fori_loop(0, 4, sides, 0)

    def finish_az(f):
        for copy in halo[f]:
            copy.wait_recv()
        az_faces(f)

    finish_az(0)
    finish_az(1)

    for copy in carried_in:
        copy.wait_recv()

    def round_into(c, carry):
        rv[c] = ibuf[c].astype(BF16).astype(F32)
        return carry

    lax.fori_loop(0, 16, round_into, 0, unroll=8)

    def corrected(m, carry):
        sums = [sol[m], None]
        for c in range(16):
            term = ibv[m, 4 * c].astype(F32) * rv[c]
            sums[c % 2] = term if sums[c % 2] is None else sums[c % 2] + term
        acc[PRESSURE, m] = sums[0] + sums[1]
        return carry

    lax.fori_loop(0, 64, corrected, 0, unroll=2)
    finish_az(2)
    finish_az(3)
    for copy in sent:
        copy.wait_send()


def held(cells):
    return pltpu.with_memory_space_constraint(cells, pltpu.HBM)


def per_device(fields, inverse_blocks, stiffness, wind_field, face_decay, wall_kind):
    hbm = pl.BlockSpec(memory_space=pltpu.HBM)
    vmem = pltpu.VMEM
    tile = (8, 128)
    lines = (GROUP, 2) + tile
    advanced = pl.pallas_call(
        kernel,
        in_specs=[hbm] * 6,
        out_specs=pl.BlockSpec(memory_space=pltpu.VMEM),
        out_shape=pltpu.VMEM((FIELDS, 64) + tile, F32),
        scratch_shapes=[
            vmem((FIELDS, 64) + tile, F32),
            vmem((64, 64) + tile, BF16),
            vmem((192, 64), BF16),
            vmem((3, 64) + tile, BF16),
            vmem((16,) + tile, F32),
            vmem((4, 128), jnp.int32),
            vmem((1536, 128), F32),
            vmem((64,) + tile, F32),
            vmem((64,) + tile, F32),
            vmem((FIELDS, 16) + tile, F32),
            vmem((FIELDS, 16) + tile, F32),
            vmem((FIELDS, 4, 4) + tile, F32),
            vmem((FIELDS,) + tile, F32),
            vmem((FIELDS,) + tile, F32),
            vmem(lines, F32),
            vmem(lines, F32),
            vmem(lines, F32),
            vmem(lines, F32),
            vmem((16,) + tile, F32),
            vmem(lines, F32),
            vmem((16,) + tile, F32),
            vmem((16,) + tile, F32),
            vmem((2,) + tile, F32),
            vmem((2,) + tile, F32),
            vmem(lines, F32),
            vmem(lines, F32),
            pltpu.SemaphoreType.DMA((6 + IB_PARTS,)),
            pltpu.SemaphoreType.DMA((49,)),
            pltpu.SemaphoreType.DMA((49,)),
        ],
        compiler_params=pltpu.CompilerParams(
            collective_id=0, has_side_effects=True, vmem_limit_bytes=50 << 20
        ),
        name="section",
    )(
        held(tiles(fields)),
        held(tiles(inverse_blocks)),
        held(stiffness.reshape(192, 64)),
        held(tiles(wind_field)),
        held(tiles(face_decay)),
        held(wall_kind.reshape(4, 128)),
    )
    return untiles(advanced)


def solution(mesh):
    placed = (
        P(None, None, "az", "rad", "ht"),
        P(None, None, "az", "rad", "ht"),
        P(),
        P(None, None, "az", "rad", "ht"),
        P(None, "az", "rad", "ht"),
        P(None, "az", "ht"),
    )
    return jax.shard_map(
        per_device,
        mesh=mesh,
        in_specs=placed,
        out_specs=P(None, None, "az", "rad", "ht"),
        check_vma=False,
    )
```

```python
import jax
import jax.numpy as jnp
from jax import lax
from jax.experimental import pallas as pl
from jax.experimental.pallas import tpu as pltpu
from jax.sharding import PartitionSpec as P

MESH = pl.DeviceIdType.MESH
F32 = jnp.float32
BF16 = jnp.bfloat16
FIELDS = 5
PRESSURE = 4
PENALTY = 2.0
TIME_STEP = 0.2
GAIN = PENALTY * TIME_STEP
GROUP = 8
EXPM1_TERMS = 11
IB_PARTS = 4
MATE_ORDER = (3, 5, 4, 1, 7, 2, 6)
PEER_ORDER = (4, 3, 5, 2, 6, 1, 7)


def tiles(cells):
    lead = cells.shape[:-3]
    n = len(lead)
    cells = cells.reshape(lead + (4, 2, 128))
    cells = cells.transpose(tuple(range(n)) + (n + 1, n, n + 2))
    return cells.reshape(lead + (8, 128))


def untiles(cells):
    lead = cells.shape[:-2]
    n = len(lead)
    cells = cells.reshape(lead + (2, 4, 128))
    cells = cells.transpose(tuple(range(n)) + (n + 1, n, n + 2))
    return cells.reshape(lead + (1, 4, 256))


def lost_share(decay):
    total = jnp.full_like(decay, 1.0)
    for term in range(EXPM1_TERMS, 1, -1):
        total = 1.0 - decay * total * (1.0 / term)
    return decay * total


def kernel(
    fields, blocks, stiff, wind, decay, walls, acc,
    fv, ibv, stv, wv, dv, kv, sl, rv, sol,
    hl, hr, rr, hp, hq, dbuf, pbuf, obuf, zbuf, ibuf, rates, share, off, pblk, oblk, wbuf, into,
    local_sem, send_sem, recv_sem, known_sem,
):
    az = lax.axis_index("az")
    rad = lax.axis_index("rad")
    ht = lax.axis_index("ht")
    count = 64
    g = lax.rem(az, GROUP)
    z = lax.div(az, GROUP)
    first = az - g
    right = {"az": lax.rem(az + 1, count)}
    left = {"az": lax.rem(az + count - 1, count)}
    other_rad = {"rad": 1 - rad}
    other_ht = {"ht": 1 - ht}
    mates = [{"az": first + lax.rem(g + k, GROUP)} for k in range(1, GROUP)]
    peers = [{"az": lax.rem(az + GROUP * k, count)} for k in range(1, 8)]

    loads = {}

    def load(name, src, dst):
        copy = pltpu.make_async_copy(src, dst, local_sem.at[len(loads)])
        loads[name] = copy
        copy.start()

    load("p", fields.at[PRESSURE], fv.at[PRESSURE])
    load("st", stiff, stv)
    load("w", wind, wv)
    load("d", decay, dv)
    load("k", walls, kv)
    load("f", fields.at[pl.ds(0, 4)], fv.at[pl.ds(0, 4)])
    rows = 64 // IB_PARTS
    for part in range(IB_PARTS):
        load("ib%d" % part, blocks.at[pl.ds(part * rows, rows)], ibv.at[pl.ds(part * rows, rows)])

    barrier = pltpu.get_barrier_semaphore()
    partners = [right, left, other_rad, other_ht, peers[0], peers[-1]] + mates
    for partner in partners:
        pl.semaphore_signal(barrier, inc=1, device_id=partner, device_id_type=MESH)

    sent = []

    def send(src, dst, partner):
        slot = len(sent)
        copy = pltpu.make_async_remote_copy(
            src_ref=src, dst_ref=dst, send_sem=send_sem.at[slot], recv_sem=recv_sem.at[slot],
            device_id=partner, device_id_type=MESH,
        )
        sent.append(copy)
        copy.start()
        return copy

    def nodes(ref, f):
        return ref.at[f].reshape(16, 4, 8, 128)

    def az_halo(f, ref=fields):
        to_right = send(nodes(ref, f).at[:, 3], hl.at[f], right)
        to_left = send(nodes(ref, f).at[:, 0], hr.at[f], left)
        return to_right, to_left

    row = lax.broadcasted_iota(jnp.int32, (8, 128), 0)
    lane = lax.broadcasted_iota(jnp.int32, (8, 128), 1)
    radius = lax.rem(row, 4)

    ht_l = 3 * (1 - ht)

    def pack(f):
        packed = jnp.zeros((8, 128), F32)
        for q in range(16):
            packed = jnp.where(lane == q + ht, pltpu.roll(fv[f, 16 * ht_l + q], q + 1, 1), packed)
        hp[f] = packed

    loads["p"].wait()
    pack(PRESSURE)
    pl.semaphore_wait(barrier, len(partners))

    for step in (0, -1):
        pl.semaphore_signal(known_sem.at[0], inc=1, device_id=peers[step], device_id_type=MESH)

    halo = {}
    rad_j = 3 * (1 - rad)
    rad_p = send(fv.at[PRESSURE].reshape(4, 4, 4, 8, 128).at[:, rad_j], rr.at[PRESSURE], other_rad)
    ht_p = send(hp.at[PRESSURE], hq.at[PRESSURE], other_ht)
    halo[PRESSURE] = az_halo(PRESSURE, fv)
    rates_in = {}
    for k in MATE_ORDER:
        mate = lax.rem(g + k, GROUP)
        rates_in[k] = send(decay.at[pl.ds(2 * mate, 2)], dbuf.at[g], mates[k - 1])
    rad_f = send(fields.at[pl.ds(0, 4)].reshape(4, 4, 4, 4, 8, 128).at[:, :, rad_j], rr.at[pl.ds(0, 4)], other_rad)

    def slopes(f):
        columns = jnp.concatenate(
            [fv.at[f].reshape(512, 128)[pl.ds(s, 64, stride=8), :].astype(BF16) for s in range(8)], axis=1
        )
        product = jnp.dot(stv[...], columns, preferred_element_type=F32)
        for s in range(8):
            sl[pl.ds(s, 192, stride=8), :] = product[:, 128 * s : 128 * (s + 1)]

        def node(n, carry):
            total = None
            for d in range(3):
                term = wv[d, n].astype(F32) * sl[pl.ds(pl.multiple_of((64 * d + n) * 8, 8), 8), :]
                total = term if total is None else total + term
            acc[f, n] = fv[f, n] - TIME_STEP * total
            return carry

        lax.fori_loop(0, 64, node, 0, unroll=8)

    def wall_codes(side):
        low = jnp.broadcast_to(kv[2 * side : 2 * side + 1, :], (8, 128))
        high = jnp.broadcast_to(kv[2 * side + 1 : 2 * side + 2, :], (8, 128))
        return jnp.where(row < 4, low, high)

    loads["st"].wait()
    loads["w"].wait()
    loads["k"].wait()
    codes = [wall_codes(0), wall_codes(1)]
    inner_row = radius == 0
    outer_row = radius == 3
    low_rows = row < 4
    is_rad0 = (row * 0 + rad) == 0
    is_ht0 = (row * 0 + ht) == 0

    def side_faces(f, is_field_2):
        factors = [
            jnp.where(code == 1, 0.0, jnp.where(code == 0, 1.0 - 2.0 * is_field_2, 1.0)) for code in codes
        ]
        for l in range(4):
            for i in range(4):
                n_in, n_out = 16 * l + i, 16 * l + 12 + i
                own_in, own_out = fv[f, n_in], fv[f, n_out]
                beside = rr[f, l, i]
                edge_in = jnp.where(is_rad0, factors[0] * own_in, pltpu.roll(beside, 5, 0))
                edge_out = jnp.where(is_rad0, pltpu.roll(beside, 3, 0), factors[1] * own_out)
                ghost_in = jnp.where(inner_row, edge_in, pltpu.roll(own_out, 1, 0))
                ghost_out = jnp.where(outer_row, edge_out, pltpu.roll(own_in, 7, 0))
                acc[f, n_in] += GAIN * (ghost_in - own_in)
                acc[f, n_out] += GAIN * (ghost_out - own_out)
        packed = hq[f]
        from_low = jnp.where(is_ht0, 0.0, packed)
        from_high = jnp.where(is_ht0, packed, 0.0)
        for q in range(16):
            own_low, own_high = fv[f, q], fv[f, 48 + q]
            turned = pltpu.roll(jnp.where(low_rows, own_high, pltpu.roll(from_low, 127 - q, 1)), 4, 0)
            ghost_low = pltpu.roll(jnp.where(lane == 127, turned, own_high), 1, 1)
            turned = pltpu.roll(jnp.where(low_rows, pltpu.roll(from_high, 127 - q, 1), own_low), 4, 0)
            ghost_high = pltpu.roll(jnp.where(lane == 0, turned, own_low), 127, 1)
            acc[f, q] += GAIN * (ghost_low - own_low)
            acc[f, 48 + q] += GAIN * (ghost_high - own_high)

    def az_faces(f):
        for q in range(16):
            acc[f, 4 * q] += GAIN * (hl[f, q] - fv[f, 4 * q])
            acc[f, 4 * q + 3] += GAIN * (hr[f, q] - fv[f, 4 * q + 3])

    slopes(PRESSURE)
    pl.semaphore_wait(known_sem.at[0], 2)
    for step in (1, -2):
        pl.semaphore_signal(known_sem.at[1], inc=1, device_id=peers[step], device_id_type=MESH)
    loads["f"].wait()
    for f in range(4):
        pack(f)
    ht_f = send(hp.at[pl.ds(0, 4)], hq.at[pl.ds(0, 4)], other_ht)
    loads["d"].wait()

    def own_share(c, carry):
        share[c] = lost_share(dv[c])
        return carry

    lax.fori_loop(0, 16, own_share, 0, unroll=4)
    rad_p.wait_recv()
    ht_p.wait_recv()
    side_faces(PRESSURE, 0.0)

    def rounded(n):
        rv[n] = acc[PRESSURE, n].astype(BF16).astype(F32)

    def product(m, start, columns):
        sums = [start, None, None, None]
        for turn, n in enumerate(columns):
            term = ibv[m, n].astype(F32) * rv[n]
            at = turn % 4
            sums[at] = term if sums[at] is None else sums[at] + term
        return (sums[0] + sums[1]) + (sums[2] + sums[3])

    inside = [n for n in range(64) if n % 4 in (1, 2)]
    beside_az = [n for n in range(64) if n % 4 in (0, 3)]
    for n in inside:
        rounded(n)
    for part in range(IB_PARTS):
        loads["ib%d" % part].wait()

    def exit_start(c, carry):
        sol[4 * c + 3] = product(4 * c + 3, None, inside)
        return carry

    lax.fori_loop(0, 16, exit_start, 0)
    for copy in halo[PRESSURE]:
        copy.wait_recv()
    az_faces(PRESSURE)
    for n in beside_az:
        rounded(n)

    def exit_row(c, carry):
        solved = product(4 * c + 3, sol[4 * c + 3], beside_az)
        sol[4 * c + 3] = solved
        off[c] = share[c] * solved
        return carry

    lax.fori_loop(0, 16, exit_row, 0)
    offsets_in = {}
    for k in MATE_ORDER:
        mate = lax.rem(g + k, GROUP)
        offsets_in[k] = send(off.at[pl.ds(2 * mate, 2)], obuf.at[g], mates[k - 1])

    for copy in rates_in.values():
        copy.wait_recv()
    dbuf[g] = dv[pl.ds(2 * g, 2)]
    passed = None
    for t in range(GROUP):
        rate = jnp.exp(-dbuf[t])
        rates[t] = rate
        passed = rate if passed is None else passed * rate
    pblk[...] = passed
    pbuf[z] = passed
    pl.semaphore_wait(known_sem.at[1], 2)
    blocks_in = [send(pblk, pbuf.at[z], peers[k - 1]) for k in PEER_ORDER]

    halo[0] = az_halo(0)

    def other_rows(c, carry):
        for i in range(3):
            sol[4 * c + i] = product(4 * c + i, None, range(64))
        return carry

    lax.fori_loop(0, 16, other_rows, 0)
    slopes(0)
    slopes(1)

    for copy in offsets_in.values():
        copy.wait_recv()
    obuf[g] = off[pl.ds(2 * g, 2)]
    state = jnp.zeros((2, 8, 128), F32)
    passed = jnp.ones((2, 8, 128), F32)
    for t in range(GROUP):
        into[t] = state
        state = rates[t] * state + obuf[t]
    oblk[...] = state
    zbuf[z] = state
    totals_in = [send(oblk, zbuf.at[z], peers[k - 1]) for k in PEER_ORDER]

    halo[1] = az_halo(1)
    halo[2] = az_halo(2)
    slopes(2)
    slopes(3)
    rad_f.wait_recv()
    ht_f.wait_recv()

    def sides(f, carry):
        side_faces(f, jnp.where(f == 2, 1.0, 0.0))
        return carry

    lax.fori_loop(0, 2, sides, 0)
    for copy in blocks_in:
        copy.wait_recv()
    whole = pbuf[0]
    for t in range(1, 8):
        whole = whole * pbuf[t]
    weight = 1.0 / (1.0 - whole)
    for k in range(1, 9):
        wbuf[k - 1] = weight
        if k < 8:
            weight = weight * pbuf[lax.rem(z + 8 - k, 8)]

    for copy in totals_in:
        copy.wait_recv()
    start = jnp.zeros((2, 8, 128), F32)
    for k in range(1, 9):
        start = start + wbuf[k - 1] * zbuf[lax.rem(z + 8 - k, 8)]
    for t in range(GROUP):
        into[t] = into[t] + passed * start
        passed = passed * rates[t]
    ibuf[pl.ds(2 * g, 2)] = into[g]
    carried_in = {}
    for k in MATE_ORDER:
        mate = lax.rem(g + k, GROUP)
        carried_in[k] = send(into.at[mate], ibuf.at[pl.ds(2 * g, 2)], mates[k - 1])
    early = len(sent)
    halo[3] = az_halo(3)
    lax.fori_loop(2, 4, sides, 0)

    def finish_az(f):
        for copy in halo[f]:
            copy.wait_recv()
        az_faces(f)

    finish_az(0)
    finish_az(1)
    finish_az(2)
    for copy in sent[:early]:
        copy.wait_send()

    def correct(source, owners):
        exits = [2 * owner + side for owner in owners for side in range(2)]
        values = [ibuf[c].astype(BF16).astype(F32) for c in exits]

        def row_of(m, carry):
            total = source(m)
            for c, value in zip(exits, values):
                total = total + ibv[m, 4 * c].astype(F32) * value
            acc[PRESSURE, m] = total
            return carry

        lax.fori_loop(0, 64, row_of, 0, unroll=4)

    correct(lambda m: sol[m], [g])
    for ks in ((2, 6), (1, 7), (4,), (3, 5)):
        for k in ks:
            carried_in[k].wait_recv()
        correct(lambda m: acc[PRESSURE, m], [lax.rem(g + GROUP - k, GROUP) for k in ks])
    finish_az(3)
    for copy in sent[early:]:
        copy.wait_send()


def held(cells):
    return pltpu.with_memory_space_constraint(cells, pltpu.HBM)


def per_device(fields, inverse_blocks, stiffness, wind_field, face_decay, wall_kind):
    hbm = pl.BlockSpec(memory_space=pltpu.HBM)
    vmem = pltpu.VMEM
    tile = (8, 128)
    lines = (GROUP, 2) + tile
    advanced = pl.pallas_call(
        kernel,
        in_specs=[hbm] * 6,
        out_specs=pl.BlockSpec(memory_space=pltpu.VMEM),
        out_shape=pltpu.VMEM((FIELDS, 64) + tile, F32),
        scratch_shapes=[
            vmem((FIELDS, 64) + tile, F32),
            vmem((64, 64) + tile, BF16),
            vmem((192, 64), BF16),
            vmem((3, 64) + tile, BF16),
            vmem((16,) + tile, F32),
            vmem((4, 128), jnp.int32),
            vmem((1536, 128), F32),
            vmem((64,) + tile, F32),
            vmem((64,) + tile, F32),
            vmem((FIELDS, 16) + tile, F32),
            vmem((FIELDS, 16) + tile, F32),
            vmem((FIELDS, 4, 4) + tile, F32),
            vmem((FIELDS,) + tile, F32),
            vmem((FIELDS,) + tile, F32),
            vmem(lines, F32),
            vmem(lines, F32),
            vmem(lines, F32),
            vmem(lines, F32),
            vmem((16,) + tile, F32),
            vmem(lines, F32),
            vmem((16,) + tile, F32),
            vmem((16,) + tile, F32),
            vmem((2,) + tile, F32),
            vmem((2,) + tile, F32),
            vmem(lines, F32),
            vmem(lines, F32),
            pltpu.SemaphoreType.DMA((6 + IB_PARTS,)),
            pltpu.SemaphoreType.DMA((49,)),
            pltpu.SemaphoreType.DMA((49,)),
            pltpu.SemaphoreType.REGULAR((2,)),
        ],
        compiler_params=pltpu.CompilerParams(
            collective_id=0, has_side_effects=True, vmem_limit_bytes=50 << 20
        ),
        name="section",
    )(
        held(tiles(fields)),
        held(tiles(inverse_blocks)),
        held(stiffness.reshape(192, 64)),
        held(tiles(wind_field)),
        held(tiles(face_decay)),
        held(wall_kind.reshape(4, 128)),
    )
    return untiles(advanced)


def solution(mesh):
    placed = (
        P(None, None, "az", "rad", "ht"),
        P(None, None, "az", "rad", "ht"),
        P(),
        P(None, None, "az", "rad", "ht"),
        P(None, "az", "rad", "ht"),
        P(None, "az", "ht"),
    )
    return jax.shard_map(
        per_device,
        mesh=mesh,
        in_specs=placed,
        out_specs=P(None, None, "az", "rad", "ht"),
        check_vma=False,
    )
```

```python
import jax
import jax.numpy as jnp
from jax import lax
from jax.experimental import pallas as pl
from jax.experimental.pallas import tpu as pltpu
from jax.sharding import PartitionSpec as P

MESH = pl.DeviceIdType.MESH
F32 = jnp.float32
BF16 = jnp.bfloat16
FIELDS = 5
PRESSURE = 4
PENALTY = 2.0
TIME_STEP = 0.2
GAIN = PENALTY * TIME_STEP
GROUP = 8
EXPM1_TERMS = 11
IB_PARTS = 4
MATE_ORDER = (3, 5, 4, 1, 7, 2, 6)
PEER_ORDER = (4, 3, 5, 2, 6, 1, 7)
BULK_SOON = ((0,), (1,), (2, 3), ())
BULK_LATE = ((), (0,), (1,), (2, 3))


def tiles(cells):
    lead = cells.shape[:-3]
    n = len(lead)
    cells = cells.reshape(lead + (4, 2, 128))
    cells = cells.transpose(tuple(range(n)) + (n + 1, n, n + 2))
    return cells.reshape(lead + (8, 128))


def untiles(cells):
    lead = cells.shape[:-2]
    n = len(lead)
    cells = cells.reshape(lead + (2, 4, 128))
    cells = cells.transpose(tuple(range(n)) + (n + 1, n, n + 2))
    return cells.reshape(lead + (1, 4, 256))


def lost_share(decay):
    total = jnp.full_like(decay, 1.0)
    for term in range(EXPM1_TERMS, 1, -1):
        total = 1.0 - decay * total * (1.0 / term)
    return decay * total


def kernel(
    fields, blocks, stiff, wind, decay, walls, acc,
    fv, ibv, stv, wv, dv, kv, sl, rv, sol,
    hl, hr, rr, hp, hq, dbuf, pbuf, obuf, zbuf, ibuf, rates, share, off, pblk, oblk, wbuf, into,
    local_sem, send_sem, recv_sem, known_sem,
):
    az = lax.axis_index("az")
    rad = lax.axis_index("rad")
    ht = lax.axis_index("ht")
    count = 64
    g = lax.rem(az, GROUP)
    z = lax.div(az, GROUP)
    first = az - g
    right = {"az": lax.rem(az + 1, count)}
    left = {"az": lax.rem(az + count - 1, count)}
    other_rad = {"rad": 1 - rad}
    other_ht = {"ht": 1 - ht}
    mates = [{"az": first + lax.rem(g + k, GROUP)} for k in range(1, GROUP)]
    peers = [{"az": lax.rem(az + GROUP * k, count)} for k in range(1, 8)]

    loads = {}

    def load(name, src, dst):
        copy = pltpu.make_async_copy(src, dst, local_sem.at[len(loads)])
        loads[name] = copy
        copy.start()

    load("p", fields.at[PRESSURE], fv.at[PRESSURE])
    load("st", stiff, stv)
    load("w", wind, wv)
    load("d", decay, dv)
    load("k", walls, kv)
    load("f", fields.at[pl.ds(0, 4)], fv.at[pl.ds(0, 4)])
    rows = 64 // IB_PARTS
    for part in range(IB_PARTS):
        load("ib%d" % part, blocks.at[pl.ds(part * rows, rows)], ibv.at[pl.ds(part * rows, rows)])

    barrier = pltpu.get_barrier_semaphore()
    partners = [right, left, other_rad, other_ht, peers[0], peers[-1]] + mates
    for partner in partners:
        pl.semaphore_signal(barrier, inc=1, device_id=partner, device_id_type=MESH)

    sent = []

    def send(src, dst, partner, begin=True):
        slot = len(sent)
        copy = pltpu.make_async_remote_copy(
            src_ref=src, dst_ref=dst, send_sem=send_sem.at[slot], recv_sem=recv_sem.at[slot],
            device_id=partner, device_id_type=MESH,
        )
        sent.append(copy)
        if begin:
            copy.start()
        return copy

    def nodes(ref, f):
        return ref.at[f].reshape(16, 4, 8, 128)

    def az_halo(f, ref, begin=True):
        to_right = send(nodes(ref, f).at[:, 3], hl.at[f], right, begin)
        to_left = send(nodes(ref, f).at[:, 0], hr.at[f], left, begin)
        return to_right, to_left

    row = lax.broadcasted_iota(jnp.int32, (8, 128), 0)
    lane = lax.broadcasted_iota(jnp.int32, (8, 128), 1)
    radius = lax.rem(row, 4)

    ht_l = 3 * (1 - ht)

    def pack(f):
        packed = jnp.zeros((8, 128), F32)
        for q in range(16):
            packed = jnp.where(lane == q + ht, pltpu.roll(fv[f, 16 * ht_l + q], q + 1, 1), packed)
        hp[f] = packed

    loads["p"].wait()
    pack(PRESSURE)
    pl.semaphore_wait(barrier, len(partners))

    for step in (0, -1):
        pl.semaphore_signal(known_sem.at[0], inc=1, device_id=peers[step], device_id_type=MESH)

    halo = {}
    rad_j = 3 * (1 - rad)
    rad_p = send(fv.at[PRESSURE].reshape(4, 4, 4, 8, 128).at[:, rad_j], rr.at[PRESSURE], other_rad)
    ht_p = send(hp.at[PRESSURE], hq.at[PRESSURE], other_ht)
    halo[PRESSURE] = az_halo(PRESSURE, fv)
    rates_in = {}
    for k in MATE_ORDER:
        mate = lax.rem(g + k, GROUP)
        rates_in[k] = send(decay.at[pl.ds(2 * mate, 2)], dbuf.at[g], mates[k - 1])
    rad_f = send(fields.at[pl.ds(0, 4)].reshape(4, 4, 4, 4, 8, 128).at[:, :, rad_j], rr.at[pl.ds(0, 4)], other_rad)

    for f in range(4):
        halo[f] = az_halo(f, fields, False)
    soon = jnp.minimum(z, 8 - z) <= 2

    def bulk(stage):
        for turn, plan in ((soon, BULK_SOON), (jnp.logical_not(soon), BULK_LATE)):
            if plan[stage]:

                @pl.when(turn)
                def _():
                    for f in plan[stage]:
                        for copy in halo[f]:
                            copy.start()

    def slopes(f):
        columns = jnp.concatenate(
            [fv.at[f].reshape(512, 128)[pl.ds(s, 64, stride=8), :].astype(BF16) for s in range(8)], axis=1
        )
        product = jnp.dot(stv[...], columns, preferred_element_type=F32)
        for s in range(8):
            sl[pl.ds(s, 192, stride=8), :] = product[:, 128 * s : 128 * (s + 1)]

        def node(n, carry):
            total = None
            for d in range(3):
                term = wv[d, n].astype(F32) * sl[pl.ds(pl.multiple_of((64 * d + n) * 8, 8), 8), :]
                total = term if total is None else total + term
            acc[f, n] = fv[f, n] - TIME_STEP * total
            return carry

        lax.fori_loop(0, 64, node, 0, unroll=8)

    def wall_codes(side):
        low = jnp.broadcast_to(kv[2 * side : 2 * side + 1, :], (8, 128))
        high = jnp.broadcast_to(kv[2 * side + 1 : 2 * side + 2, :], (8, 128))
        return jnp.where(row < 4, low, high)

    loads["st"].wait()
    loads["w"].wait()
    loads["k"].wait()
    codes = [wall_codes(0), wall_codes(1)]
    inner_row = radius == 0
    outer_row = radius == 3
    low_rows = row < 4
    is_rad0 = (row * 0 + rad) == 0
    is_ht0 = (row * 0 + ht) == 0

    def side_faces(f, is_field_2):
        factors = [
            jnp.where(code == 1, 0.0, jnp.where(code == 0, 1.0 - 2.0 * is_field_2, 1.0)) for code in codes
        ]
        for l in range(4):
            for i in range(4):
                n_in, n_out = 16 * l + i, 16 * l + 12 + i
                own_in, own_out = fv[f, n_in], fv[f, n_out]
                beside = rr[f, l, i]
                edge_in = jnp.where(is_rad0, factors[0] * own_in, pltpu.roll(beside, 5, 0))
                edge_out = jnp.where(is_rad0, pltpu.roll(beside, 3, 0), factors[1] * own_out)
                ghost_in = jnp.where(inner_row, edge_in, pltpu.roll(own_out, 1, 0))
                ghost_out = jnp.where(outer_row, edge_out, pltpu.roll(own_in, 7, 0))
                acc[f, n_in] += GAIN * (ghost_in - own_in)
                acc[f, n_out] += GAIN * (ghost_out - own_out)
        packed = hq[f]
        from_low = jnp.where(is_ht0, 0.0, packed)
        from_high = jnp.where(is_ht0, packed, 0.0)
        for q in range(16):
            own_low, own_high = fv[f, q], fv[f, 48 + q]
            turned = pltpu.roll(jnp.where(low_rows, own_high, pltpu.roll(from_low, 127 - q, 1)), 4, 0)
            ghost_low = pltpu.roll(jnp.where(lane == 127, turned, own_high), 1, 1)
            turned = pltpu.roll(jnp.where(low_rows, pltpu.roll(from_high, 127 - q, 1), own_low), 4, 0)
            ghost_high = pltpu.roll(jnp.where(lane == 0, turned, own_low), 127, 1)
            acc[f, q] += GAIN * (ghost_low - own_low)
            acc[f, 48 + q] += GAIN * (ghost_high - own_high)

    def az_faces(f):
        for q in range(16):
            acc[f, 4 * q] += GAIN * (hl[f, q] - fv[f, 4 * q])
            acc[f, 4 * q + 3] += GAIN * (hr[f, q] - fv[f, 4 * q + 3])

    slopes(PRESSURE)
    bulk(0)
    pl.semaphore_wait(known_sem.at[0], 2)
    for step in (1, -2):
        pl.semaphore_signal(known_sem.at[1], inc=1, device_id=peers[step], device_id_type=MESH)
    loads["f"].wait()
    for f in range(4):
        pack(f)
    ht_f = send(hp.at[pl.ds(0, 4)], hq.at[pl.ds(0, 4)], other_ht)
    loads["d"].wait()

    def own_share(c, carry):
        share[c] = lost_share(dv[c])
        return carry

    lax.fori_loop(0, 16, own_share, 0, unroll=4)
    rad_p.wait_recv()
    ht_p.wait_recv()
    side_faces(PRESSURE, 0.0)

    def rounded(n):
        rv[n] = acc[PRESSURE, n].astype(BF16).astype(F32)

    def product(m, start, columns):
        sums = [start, None, None, None]
        for turn, n in enumerate(columns):
            term = ibv[m, n].astype(F32) * rv[n]
            at = turn % 4
            sums[at] = term if sums[at] is None else sums[at] + term
        return (sums[0] + sums[1]) + (sums[2] + sums[3])

    inside = [n for n in range(64) if n % 4 in (1, 2)]
    beside_az = [n for n in range(64) if n % 4 in (0, 3)]
    for n in inside:
        rounded(n)
    for part in range(IB_PARTS):
        loads["ib%d" % part].wait()

    def exit_start(c, carry):
        sol[4 * c + 3] = product(4 * c + 3, None, inside)
        return carry

    lax.fori_loop(0, 16, exit_start, 0)
    for copy in halo[PRESSURE]:
        copy.wait_recv()
    az_faces(PRESSURE)
    for n in beside_az:
        rounded(n)

    def exit_row(c, carry):
        solved = product(4 * c + 3, sol[4 * c + 3], beside_az)
        sol[4 * c + 3] = solved
        off[c] = share[c] * solved
        return carry

    lax.fori_loop(0, 16, exit_row, 0)
    offsets_in = {}
    for k in MATE_ORDER:
        mate = lax.rem(g + k, GROUP)
        offsets_in[k] = send(off.at[pl.ds(2 * mate, 2)], obuf.at[g], mates[k - 1])

    for copy in rates_in.values():
        copy.wait_recv()
    dbuf[g] = dv[pl.ds(2 * g, 2)]
    passed = None
    for t in range(GROUP):
        rate = jnp.exp(-dbuf[t])
        rates[t] = rate
        passed = rate if passed is None else passed * rate
    pblk[...] = passed
    pbuf[z] = passed
    pl.semaphore_wait(known_sem.at[1], 2)
    blocks_in = [send(pblk, pbuf.at[z], peers[k - 1]) for k in PEER_ORDER]

    bulk(1)

    def other_rows(c, carry):
        for i in range(3):
            sol[4 * c + i] = product(4 * c + i, None, range(64))
        return carry

    lax.fori_loop(0, 16, other_rows, 0)
    slopes(0)
    slopes(1)

    for copy in offsets_in.values():
        copy.wait_recv()
    obuf[g] = off[pl.ds(2 * g, 2)]
    state = jnp.zeros((2, 8, 128), F32)
    passed = jnp.ones((2, 8, 128), F32)
    for t in range(GROUP):
        into[t] = state
        state = rates[t] * state + obuf[t]
    oblk[...] = state
    zbuf[z] = state
    totals_in = [send(oblk, zbuf.at[z], peers[k - 1]) for k in PEER_ORDER]

    bulk(2)
    slopes(2)
    slopes(3)
    rad_f.wait_recv()
    ht_f.wait_recv()

    def sides(f, carry):
        side_faces(f, jnp.where(f == 2, 1.0, 0.0))
        return carry

    lax.fori_loop(0, 2, sides, 0)
    for copy in blocks_in:
        copy.wait_recv()
    whole = pbuf[0]
    for t in range(1, 8):
        whole = whole * pbuf[t]
    weight = 1.0 / (1.0 - whole)
    for k in range(1, 9):
        wbuf[k - 1] = weight
        if k < 8:
            weight = weight * pbuf[lax.rem(z + 8 - k, 8)]

    for copy in totals_in:
        copy.wait_recv()
    start = jnp.zeros((2, 8, 128), F32)
    for k in range(1, 9):
        start = start + wbuf[k - 1] * zbuf[lax.rem(z + 8 - k, 8)]
    for t in range(GROUP):
        into[t] = into[t] + passed * start
        passed = passed * rates[t]
    ibuf[pl.ds(2 * g, 2)] = into[g]
    carried_in = {}
    for k in MATE_ORDER:
        mate = lax.rem(g + k, GROUP)
        carried_in[k] = send(into.at[mate], ibuf.at[pl.ds(2 * g, 2)], mates[k - 1])
    bulk(3)
    lax.fori_loop(2, 4, sides, 0)

    def finish_az(f):
        for copy in halo[f]:
            copy.wait_recv()
        az_faces(f)

    finish_az(0)
    finish_az(1)
    finish_az(2)
    def correct(source, owners):
        exits = [2 * owner + side for owner in owners for side in range(2)]
        values = [ibuf[c].astype(BF16).astype(F32) for c in exits]

        def row_of(m, carry):
            total = source(m)
            for c, value in zip(exits, values):
                total = total + ibv[m, 4 * c].astype(F32) * value
            acc[PRESSURE, m] = total
            return carry

        lax.fori_loop(0, 64, row_of, 0, unroll=4)

    correct(lambda m: sol[m], [g])
    for ks in ((2, 6), (1, 7), (4,), (3, 5)):
        for k in ks:
            carried_in[k].wait_recv()
        correct(lambda m: acc[PRESSURE, m], [lax.rem(g + GROUP - k, GROUP) for k in ks])
    finish_az(3)
    for copy in sent:
        copy.wait_send()


def held(cells):
    return pltpu.with_memory_space_constraint(cells, pltpu.HBM)


def per_device(fields, inverse_blocks, stiffness, wind_field, face_decay, wall_kind):
    hbm = pl.BlockSpec(memory_space=pltpu.HBM)
    vmem = pltpu.VMEM
    tile = (8, 128)
    lines = (GROUP, 2) + tile
    advanced = pl.pallas_call(
        kernel,
        in_specs=[hbm] * 6,
        out_specs=pl.BlockSpec(memory_space=pltpu.VMEM),
        out_shape=pltpu.VMEM((FIELDS, 64) + tile, F32),
        scratch_shapes=[
            vmem((FIELDS, 64) + tile, F32),
            vmem((64, 64) + tile, BF16),
            vmem((192, 64), BF16),
            vmem((3, 64) + tile, BF16),
            vmem((16,) + tile, F32),
            vmem((4, 128), jnp.int32),
            vmem((1536, 128), F32),
            vmem((64,) + tile, F32),
            vmem((64,) + tile, F32),
            vmem((FIELDS, 16) + tile, F32),
            vmem((FIELDS, 16) + tile, F32),
            vmem((FIELDS, 4, 4) + tile, F32),
            vmem((FIELDS,) + tile, F32),
            vmem((FIELDS,) + tile, F32),
            vmem(lines, F32),
            vmem(lines, F32),
            vmem(lines, F32),
            vmem(lines, F32),
            vmem((16,) + tile, F32),
            vmem(lines, F32),
            vmem((16,) + tile, F32),
            vmem((16,) + tile, F32),
            vmem((2,) + tile, F32),
            vmem((2,) + tile, F32),
            vmem(lines, F32),
            vmem(lines, F32),
            pltpu.SemaphoreType.DMA((6 + IB_PARTS,)),
            pltpu.SemaphoreType.DMA((49,)),
            pltpu.SemaphoreType.DMA((49,)),
            pltpu.SemaphoreType.REGULAR((2,)),
        ],
        compiler_params=pltpu.CompilerParams(
            collective_id=0, has_side_effects=True, vmem_limit_bytes=50 << 20
        ),
        name="section",
    )(
        held(tiles(fields)),
        held(tiles(inverse_blocks)),
        held(stiffness.reshape(192, 64)),
        held(tiles(wind_field)),
        held(tiles(face_decay)),
        held(wall_kind.reshape(4, 128)),
    )
    return untiles(advanced)


def solution(mesh):
    placed = (
        P(None, None, "az", "rad", "ht"),
        P(None, None, "az", "rad", "ht"),
        P(),
        P(None, None, "az", "rad", "ht"),
        P(None, "az", "rad", "ht"),
        P(None, "az", "ht"),
    )
    return jax.shard_map(
        per_device,
        mesh=mesh,
        in_specs=placed,
        out_specs=P(None, None, "az", "rad", "ht"),
        check_vma=False,
    )
```

```python
import jax
import jax.numpy as jnp
from jax import lax
from jax.experimental import pallas as pl
from jax.experimental.pallas import tpu as pltpu
from jax.sharding import PartitionSpec as P

MESH = pl.DeviceIdType.MESH
F32 = jnp.float32
BF16 = jnp.bfloat16
FIELDS = 5
PRESSURE = 4
PENALTY = 2.0
TIME_STEP = 0.2
GAIN = PENALTY * TIME_STEP
GROUP = 8
EXPM1_TERMS = 11
IB_PARTS = 4
MATE_ORDER = (3, 5, 4, 1, 7, 2, 6)
PEER_ORDER = (4, 3, 5, 2, 6, 1, 7)
BULK_SOON = ((0,), (1,), (2, 3), ())
BULK_LATE = ((), (0,), (1,), (2, 3))


def tiles(cells):
    lead = cells.shape[:-3]
    n = len(lead)
    cells = cells.reshape(lead + (4, 2, 128))
    cells = cells.transpose(tuple(range(n)) + (n + 1, n, n + 2))
    return cells.reshape(lead + (8, 128))


def untiles(cells):
    lead = cells.shape[:-2]
    n = len(lead)
    cells = cells.reshape(lead + (2, 4, 128))
    cells = cells.transpose(tuple(range(n)) + (n + 1, n, n + 2))
    return cells.reshape(lead + (1, 4, 256))


def lost_share(decay):
    total = jnp.full_like(decay, 1.0)
    for term in range(EXPM1_TERMS, 1, -1):
        total = 1.0 - decay * total * (1.0 / term)
    return decay * total


def kernel(
    fields, blocks, stiff, wind, decay, walls, acc,
    fv, ibv, stv, wv, dv, kv, sl, rv, sol,
    hl, hr, rr, hp, hq, dbuf, pbuf, obuf, zbuf, ibuf, rates, share, off, pblk, oblk, wbuf, into,
    local_sem, send_sem, recv_sem, known_sem,
):
    az = lax.axis_index("az")
    rad = lax.axis_index("rad")
    ht = lax.axis_index("ht")
    count = 64
    g = lax.rem(az, GROUP)
    z = lax.div(az, GROUP)
    first = az - g
    right = {"az": lax.rem(az + 1, count)}
    left = {"az": lax.rem(az + count - 1, count)}
    other_rad = {"rad": 1 - rad}
    other_ht = {"ht": 1 - ht}
    mates = [{"az": first + lax.rem(g + k, GROUP)} for k in range(1, GROUP)]
    peers = [{"az": lax.rem(az + GROUP * k, count)} for k in range(1, 8)]

    loads = {}

    def load(name, src, dst):
        copy = pltpu.make_async_copy(src, dst, local_sem.at[len(loads)])
        loads[name] = copy
        copy.start()

    load("p", fields.at[PRESSURE], fv.at[PRESSURE])
    load("st", stiff, stv)
    load("w", wind, wv)
    load("d", decay, dv)
    load("k", walls, kv)
    load("f", fields.at[pl.ds(0, 4)], fv.at[pl.ds(0, 4)])
    rows = 64 // IB_PARTS
    for part in range(IB_PARTS):
        load("ib%d" % part, blocks.at[pl.ds(part * rows, rows)], ibv.at[pl.ds(part * rows, rows)])

    barrier = pltpu.get_barrier_semaphore()
    partners = [right, left, other_rad, other_ht, peers[0], peers[-1]] + mates
    for partner in partners:
        pl.semaphore_signal(barrier, inc=1, device_id=partner, device_id_type=MESH)

    sent = []

    def send(src, dst, partner, begin=True):
        slot = len(sent)
        copy = pltpu.make_async_remote_copy(
            src_ref=src, dst_ref=dst, send_sem=send_sem.at[slot], recv_sem=recv_sem.at[slot],
            device_id=partner, device_id_type=MESH,
        )
        sent.append(copy)
        if begin:
            copy.start()
        return copy

    def nodes(ref, f):
        return ref.at[f].reshape(16, 4, 8, 128)

    def az_halo(f, ref, begin=True):
        to_right = send(nodes(ref, f).at[:, 3], hl.at[f], right, begin)
        to_left = send(nodes(ref, f).at[:, 0], hr.at[f], left, begin)
        return to_right, to_left

    row = lax.broadcasted_iota(jnp.int32, (8, 128), 0)
    lane = lax.broadcasted_iota(jnp.int32, (8, 128), 1)
    radius = lax.rem(row, 4)

    ht_l = 3 * (1 - ht)

    def pack(f):
        packed = jnp.zeros((8, 128), F32)
        for q in range(16):
            packed = jnp.where(lane == q + ht, pltpu.roll(fv[f, 16 * ht_l + q], q + 1, 1), packed)
        hp[f] = packed

    loads["p"].wait()
    pack(PRESSURE)
    pl.semaphore_wait(barrier, len(partners))

    for step in (0, -1):
        pl.semaphore_signal(known_sem.at[0], inc=1, device_id=peers[step], device_id_type=MESH)

    halo = {}
    rad_j = 3 * (1 - rad)
    rad_p = send(fv.at[PRESSURE].reshape(4, 4, 4, 8, 128).at[:, rad_j], rr.at[PRESSURE], other_rad)
    ht_p = send(hp.at[PRESSURE], hq.at[PRESSURE], other_ht)
    halo[PRESSURE] = az_halo(PRESSURE, fv, False)

    @pl.when(rad == 0)
    def _():
        for copy in halo[PRESSURE][::-1]:
            copy.start()

    @pl.when(rad == 1)
    def _():
        for copy in halo[PRESSURE]:
            copy.start()

    rates_in = {}
    for k in MATE_ORDER:
        mate = lax.rem(g + k, GROUP)
        rates_in[k] = send(decay.at[pl.ds(2 * mate, 2)], dbuf.at[g], mates[k - 1])
    rad_f = send(fields.at[pl.ds(0, 4)].reshape(4, 4, 4, 4, 8, 128).at[:, :, rad_j], rr.at[pl.ds(0, 4)], other_rad)

    for f in range(4):
        halo[f] = az_halo(f, fields, False)
    soon = jnp.minimum(z, 8 - z) <= 2

    def bulk(stage):
        for turn, plan in ((soon, BULK_SOON), (jnp.logical_not(soon), BULK_LATE)):
            if plan[stage]:

                @pl.when(turn)
                def _():
                    for f in plan[stage]:
                        for copy in halo[f]:
                            copy.start()

    def slopes(f):
        columns = jnp.concatenate(
            [fv.at[f].reshape(512, 128)[pl.ds(s, 64, stride=8), :].astype(BF16) for s in range(8)], axis=1
        )
        product = jnp.dot(stv[...], columns, preferred_element_type=F32)
        for s in range(8):
            sl[pl.ds(s, 192, stride=8), :] = product[:, 128 * s : 128 * (s + 1)]

        def node(n, carry):
            total = None
            for d in range(3):
                term = wv[d, n].astype(F32) * sl[pl.ds(pl.multiple_of((64 * d + n) * 8, 8), 8), :]
                total = term if total is None else total + term
            acc[f, n] = fv[f, n] - TIME_STEP * total
            return carry

        lax.fori_loop(0, 64, node, 0, unroll=8)

    def wall_codes(side):
        low = jnp.broadcast_to(kv[2 * side : 2 * side + 1, :], (8, 128))
        high = jnp.broadcast_to(kv[2 * side + 1 : 2 * side + 2, :], (8, 128))
        return jnp.where(row < 4, low, high)

    loads["st"].wait()
    loads["w"].wait()
    loads["k"].wait()
    codes = [wall_codes(0), wall_codes(1)]
    inner_row = radius == 0
    outer_row = radius == 3
    low_rows = row < 4
    is_rad0 = (row * 0 + rad) == 0
    is_ht0 = (row * 0 + ht) == 0

    def side_faces(f, is_field_2):
        factors = [
            jnp.where(code == 1, 0.0, jnp.where(code == 0, 1.0 - 2.0 * is_field_2, 1.0)) for code in codes
        ]
        for l in range(4):
            for i in range(4):
                n_in, n_out = 16 * l + i, 16 * l + 12 + i
                own_in, own_out = fv[f, n_in], fv[f, n_out]
                beside = rr[f, l, i]
                edge_in = jnp.where(is_rad0, factors[0] * own_in, pltpu.roll(beside, 5, 0))
                edge_out = jnp.where(is_rad0, pltpu.roll(beside, 3, 0), factors[1] * own_out)
                ghost_in = jnp.where(inner_row, edge_in, pltpu.roll(own_out, 1, 0))
                ghost_out = jnp.where(outer_row, edge_out, pltpu.roll(own_in, 7, 0))
                acc[f, n_in] += GAIN * (ghost_in - own_in)
                acc[f, n_out] += GAIN * (ghost_out - own_out)
        packed = hq[f]
        from_low = jnp.where(is_ht0, 0.0, packed)
        from_high = jnp.where(is_ht0, packed, 0.0)
        for q in range(16):
            own_low, own_high = fv[f, q], fv[f, 48 + q]
            turned = pltpu.roll(jnp.where(low_rows, own_high, pltpu.roll(from_low, 127 - q, 1)), 4, 0)
            ghost_low = pltpu.roll(jnp.where(lane == 127, turned, own_high), 1, 1)
            turned = pltpu.roll(jnp.where(low_rows, pltpu.roll(from_high, 127 - q, 1), own_low), 4, 0)
            ghost_high = pltpu.roll(jnp.where(lane == 0, turned, own_low), 127, 1)
            acc[f, q] += GAIN * (ghost_low - own_low)
            acc[f, 48 + q] += GAIN * (ghost_high - own_high)

    def az_faces(f):
        for q in range(16):
            acc[f, 4 * q] += GAIN * (hl[f, q] - fv[f, 4 * q])
            acc[f, 4 * q + 3] += GAIN * (hr[f, q] - fv[f, 4 * q + 3])

    slopes(PRESSURE)
    bulk(0)
    pl.semaphore_wait(known_sem.at[0], 2)
    for step in (1, -2):
        pl.semaphore_signal(known_sem.at[1], inc=1, device_id=peers[step], device_id_type=MESH)
    loads["f"].wait()
    for f in range(4):
        pack(f)
    ht_f = send(hp.at[pl.ds(0, 4)], hq.at[pl.ds(0, 4)], other_ht)
    loads["d"].wait()

    def own_share(c, carry):
        share[c] = lost_share(dv[c])
        return carry

    lax.fori_loop(0, 16, own_share, 0, unroll=4)
    rad_p.wait_recv()
    ht_p.wait_recv()
    side_faces(PRESSURE, 0.0)

    def rounded(n):
        rv[n] = acc[PRESSURE, n].astype(BF16).astype(F32)

    def product(m, start, columns):
        sums = [start, None, None, None]
        for turn, n in enumerate(columns):
            term = ibv[m, n].astype(F32) * rv[n]
            at = turn % 4
            sums[at] = term if sums[at] is None else sums[at] + term
        return (sums[0] + sums[1]) + (sums[2] + sums[3])

    inside = [n for n in range(64) if n % 4 in (1, 2)]
    beside_az = [n for n in range(64) if n % 4 in (0, 3)]
    for n in inside:
        rounded(n)
    for part in range(IB_PARTS):
        loads["ib%d" % part].wait()

    def exit_start(c, carry):
        sol[4 * c + 3] = product(4 * c + 3, None, inside)
        return carry

    lax.fori_loop(0, 16, exit_start, 0)
    for copy in halo[PRESSURE]:
        copy.wait_recv()
    az_faces(PRESSURE)
    for n in beside_az:
        rounded(n)

    def exit_row(c, carry):
        solved = product(4 * c + 3, sol[4 * c + 3], beside_az)
        sol[4 * c + 3] = solved
        off[c] = share[c] * solved
        return carry

    lax.fori_loop(0, 16, exit_row, 0)
    offsets_in = {}
    for k in MATE_ORDER:
        mate = lax.rem(g + k, GROUP)
        offsets_in[k] = send(off.at[pl.ds(2 * mate, 2)], obuf.at[g], mates[k - 1])

    for copy in rates_in.values():
        copy.wait_recv()
    dbuf[g] = dv[pl.ds(2 * g, 2)]
    passed = None
    for t in range(GROUP):
        rate = jnp.exp(-dbuf[t])
        rates[t] = rate
        passed = rate if passed is None else passed * rate
    pblk[...] = passed
    pbuf[z] = passed
    pl.semaphore_wait(known_sem.at[1], 2)
    blocks_in = [send(pblk, pbuf.at[z], peers[k - 1]) for k in PEER_ORDER]

    bulk(1)

    def other_rows(c, carry):
        for i in range(3):
            sol[4 * c + i] = product(4 * c + i, None, range(64))
        return carry

    lax.fori_loop(0, 16, other_rows, 0)
    slopes(0)
    slopes(1)

    for copy in offsets_in.values():
        copy.wait_recv()
    obuf[g] = off[pl.ds(2 * g, 2)]
    state = jnp.zeros((2, 8, 128), F32)
    passed = jnp.ones((2, 8, 128), F32)
    for t in range(GROUP):
        into[t] = state
        state = rates[t] * state + obuf[t]
    oblk[...] = state
    zbuf[z] = state
    totals_in = [send(oblk, zbuf.at[z], peers[k - 1]) for k in PEER_ORDER]

    bulk(2)
    slopes(2)
    slopes(3)
    rad_f.wait_recv()
    ht_f.wait_recv()

    def sides(f, carry):
        side_faces(f, jnp.where(f == 2, 1.0, 0.0))
        return carry

    lax.fori_loop(0, 2, sides, 0)
    for copy in blocks_in:
        copy.wait_recv()
    whole = pbuf[0]
    for t in range(1, 8):
        whole = whole * pbuf[t]
    weight = 1.0 / (1.0 - whole)
    for k in range(1, 9):
        wbuf[k - 1] = weight
        if k < 8:
            weight = weight * pbuf[lax.rem(z + 8 - k, 8)]

    for copy in totals_in:
        copy.wait_recv()
    start = jnp.zeros((2, 8, 128), F32)
    for k in range(1, 9):
        start = start + wbuf[k - 1] * zbuf[lax.rem(z + 8 - k, 8)]
    for t in range(GROUP):
        into[t] = into[t] + passed * start
        passed = passed * rates[t]
    ibuf[pl.ds(2 * g, 2)] = into[g]
    carried_in = {}
    for k in MATE_ORDER:
        mate = lax.rem(g + k, GROUP)
        carried_in[k] = send(into.at[mate], ibuf.at[pl.ds(2 * g, 2)], mates[k - 1])
    bulk(3)
    lax.fori_loop(2, 4, sides, 0)

    def finish_az(f):
        for copy in halo[f]:
            copy.wait_recv()
        az_faces(f)

    finish_az(0)
    finish_az(1)
    finish_az(2)
    def correct(source, owners):
        exits = [2 * owner + side for owner in owners for side in range(2)]
        values = [ibuf[c].astype(BF16).astype(F32) for c in exits]

        def row_of(m, carry):
            total = source(m)
            for c, value in zip(exits, values):
                total = total + ibv[m, 4 * c].astype(F32) * value
            acc[PRESSURE, m] = total
            return carry

        lax.fori_loop(0, 64, row_of, 0, unroll=4)

    correct(lambda m: sol[m], [g])
    for ks in ((2, 6), (1, 7), (4,), (3, 5)):
        for k in ks:
            carried_in[k].wait_recv()
        correct(lambda m: acc[PRESSURE, m], [lax.rem(g + GROUP - k, GROUP) for k in ks])
    finish_az(3)
    for copy in sent:
        copy.wait_send()


def held(cells):
    return pltpu.with_memory_space_constraint(cells, pltpu.HBM)


def per_device(fields, inverse_blocks, stiffness, wind_field, face_decay, wall_kind):
    hbm = pl.BlockSpec(memory_space=pltpu.HBM)
    vmem = pltpu.VMEM
    tile = (8, 128)
    lines = (GROUP, 2) + tile
    advanced = pl.pallas_call(
        kernel,
        in_specs=[hbm] * 6,
        out_specs=pl.BlockSpec(memory_space=pltpu.VMEM),
        out_shape=pltpu.VMEM((FIELDS, 64) + tile, F32),
        scratch_shapes=[
            vmem((FIELDS, 64) + tile, F32),
            vmem((64, 64) + tile, BF16),
            vmem((192, 64), BF16),
            vmem((3, 64) + tile, BF16),
            vmem((16,) + tile, F32),
            vmem((4, 128), jnp.int32),
            vmem((1536, 128), F32),
            vmem((64,) + tile, F32),
            vmem((64,) + tile, F32),
            vmem((FIELDS, 16) + tile, F32),
            vmem((FIELDS, 16) + tile, F32),
            vmem((FIELDS, 4, 4) + tile, F32),
            vmem((FIELDS,) + tile, F32),
            vmem((FIELDS,) + tile, F32),
            vmem(lines, F32),
            vmem(lines, F32),
            vmem(lines, F32),
            vmem(lines, F32),
            vmem((16,) + tile, F32),
            vmem(lines, F32),
            vmem((16,) + tile, F32),
            vmem((16,) + tile, F32),
            vmem((2,) + tile, F32),
            vmem((2,) + tile, F32),
            vmem(lines, F32),
            vmem(lines, F32),
            pltpu.SemaphoreType.DMA((6 + IB_PARTS,)),
            pltpu.SemaphoreType.DMA((49,)),
            pltpu.SemaphoreType.DMA((49,)),
            pltpu.SemaphoreType.REGULAR((2,)),
        ],
        compiler_params=pltpu.CompilerParams(
            collective_id=0, has_side_effects=True, vmem_limit_bytes=50 << 20
        ),
        name="section",
    )(
        held(tiles(fields)),
        held(tiles(inverse_blocks)),
        held(stiffness.reshape(192, 64)),
        held(tiles(wind_field)),
        held(tiles(face_decay)),
        held(wall_kind.reshape(4, 128)),
    )
    return untiles(advanced)


def solution(mesh):
    placed = (
        P(None, None, "az", "rad", "ht"),
        P(None, None, "az", "rad", "ht"),
        P(),
        P(None, None, "az", "rad", "ht"),
        P(None, "az", "rad", "ht"),
        P(None, "az", "ht"),
    )
    return jax.shard_map(
        per_device,
        mesh=mesh,
        in_specs=placed,
        out_specs=P(None, None, "az", "rad", "ht"),
        check_vma=False,
    )
```
